32 devices in a mesh: dp: 8 (over z, y), tensor: 4 (over x, core).
Axes of the slice: x: 2, y: 2, z: 4, core: 2. Of those that a mesh axis runs over, the one named last changes fastest.
Arguments:
- block_input: bfloat16 [8192, 768], P(('dp', 'tensor')), may hold values from -6 to 6
- cotangent: bfloat16 [8192, 768], P(('dp', 'tensor')), may hold values from -6 to 6
- lengths: int32 [8], P('dp'), may hold values from 512 to 1024, as said below
- routes: int32 [8192, 2], P('dp'), may hold values from 0 to 63, all different within a row; in each aligned block of 1024 rows (0 to 1023, 1024 to 2047, ...) at most 48 rows name the same one
- buckets: int32 [1024], replicated, may hold values from 0 to 31
- attn_gain: bfloat16 [768], replicated, may hold values from 0.25 to 1.75
- moe_gain: bfloat16 [768], replicated, may hold values from 0.25 to 1.75
- query_weight: bfloat16 [768, 768], P(None, 'tensor'), may hold values from -0.21875 to 0.21875
- key_weight: bfloat16 [768, 768], P(None, 'tensor'), may hold values from -0.21875 to 0.21875
- value_weight: bfloat16 [768, 768], P(None, 'tensor'), may hold values from -0.21875 to 0.21875
- output_weight: bfloat16 [768, 768], P('tensor'), may hold values from -0.875 to 0.875
- bias_table: bfloat16 [32, 12], P(None, 'tensor'), may hold values from -4 to 4
- router_weight: bfloat16 [768, 64], replicated, may hold values from -0.21875 to 0.21875
- expert_in: bfloat16 [64, 768, 3072], P('dp', None, 'tensor'), may hold values from -0.21875 to 0.21875
- expert_out: bfloat16 [64, 3072, 768], P('dp', 'tensor'), may hold values from -0.21875 to 0.21875
Outputs:
- block_output: float32 [8192, 768], P(('dp', 'tensor'))
- input_grad: float32 [8192, 768], P(('dp', 'tensor'))
- attn_gain_grad: float32 [768], P('tensor')
- moe_gain_grad: float32 [768], P('tensor')
- query_grad: float32 [768, 768], P(None, 'tensor')
- key_grad: float32 [768, 768], P(None, 'tensor')
- value_grad: float32 [768, 768], P(None, 'tensor')
- output_grad: float32 [768, 768], P('tensor')
- table_grad: float32 [32, 12], P(None, 'tensor')
- router_grad: float32 [768, 64], P('tensor')
- expert_in_grad: float32 [64, 768, 3072], P('dp', None, 'tensor')
- expert_out_grad: float32 [64, 3072, 768], P('dp', 'tensor')
The draws below stay inside these ranges and needn't reach their ends.
Inputs may be any that keep to these rules, and one draw needn't show every extreme that they name: `lengths`: every sequence's valid slots form a prefix of its 1024 slots. `routes`: the two entries of a row differ. In each aligned block of 1024 rows (the rows of one index of dp) no expert is named by more than 48 rows. `buckets`: an arbitrary map; neighbouring distances need not share a bucket.
All inputs are finite; a program needn't handle non-finite values.
Results may differ from the reference program's by a relative error of at most 0.017.
Values may be sent and summed in bfloat16 or wider, within the bound.
No kernel may reach another device: no remote copies, remote signals or barrier semaphores. Data moves between devices by JAX's collectives and lax.ppermute only.
A program may use at most 192 MiB of HBM per device.

```python
import math
import jax
import jax.numpy as jnp
import numpy as np
from jax import lax

D = 768
H = 12
HD = 64
FF = 3072
EXPERTS = 64
NB = 32
SEQ = 1024
SEQS = 8
ROWS = 1024
TOKENS = 8192
CAP = 48
N_DP = 8
N_TENSOR = 4


def draw_lengths(key, part):
    first_key, second_key, third_key = jax.random.split(key, 3)
    values = jax.random.randint(first_key, (SEQS,), SEQ // 2, SEQ + 1)
    longest = jax.random.randint(second_key, (), 0, SEQS)
    shortest = (longest + 1 + jax.random.randint(third_key, (), 0, SEQS - 1)) % SEQS
    values = values.at[longest].set(SEQ)
    values = values.at[shortest].set(SEQ // 2)
    return values.astype(jnp.int32)


def place_ends(entries, stream_key, low, top_value):
    index_at = [jax.random.randint(jax.random.fold_in(stream_key, axis), (), 0, length) for axis, length in enumerate(entries.shape)]
    widest = entries.shape.index(max(entries.shape))
    next_to = index_at[:widest] + [(index_at[widest] + 1) % entries.shape[widest]] + index_at[widest + 1:]
    return entries.at[tuple(index_at)].set(low).at[tuple(next_to)].set(top_value)


def block_scale(rng, extent, cuts, smallest, top_value):
    def one(dim, shards_of):
        draws = jax.random.uniform(jax.random.fold_in(jax.random.fold_in(rng, 6), dim), (shards_of,), jnp.float32, smallest / len(cuts), top_value / len(cuts))
        return jnp.repeat(jnp.exp(draws), extent[dim] // shards_of).reshape((-1,) + (1,) * (len(extent) - dim - 1))

    loudness = one(*cuts[0])
    for cut in cuts[1:]:
        loudness = loudness * one(*cut)
    return loudness


def assign_block(stream_key, own, number, rows, count, top, most, skew):
    ranking = jax.random.permutation(stream_key, count)
    heavy_load, usual = portions_of(count, rows * top, most, skew, True), portions_of(count, rows * top, most, skew, False)
    places = jnp.arange(count)

    def named(sizes, offset_by):
        used = int((sizes > 0).sum())
        fixed = max(1, used // 4)
        moved = fixed + (places - fixed + offset_by * (used - fixed)) % max(1, count - fixed)
        return jnp.zeros((count,), jnp.int32).at[ranking[jnp.where(places < fixed, places, moved)]].set(jnp.asarray(sizes, jnp.int32))

    sizes = jnp.where(number % 4 == 0, named(heavy_load, number // 4), named(usual, number - number // 4 - 1))
    mixed = jax.random.permutation(jax.random.fold_in(own, 3), count)
    source_of, taker = mixed[0:count // 2 * 2:2], mixed[1:count // 2 * 2:2]
    slack = jnp.minimum(sizes[source_of] - 1, most - sizes[taker]) // 2
    slack = jnp.where((source_of == ranking[0]) | (taker == ranking[0]) | (sizes[taker] == 0), 0, jnp.maximum(slack, 0))
    moved = jax.random.randint(jax.random.fold_in(own, 4), (count // 2,), 0, 1 << 20) % (slack + 1)
    sizes = sizes.at[source_of].add(-moved).at[taker].add(moved)
    labels = jnp.searchsorted(jnp.cumsum(sizes), jnp.arange(rows * top), side="right").astype(jnp.int32)
    grid = labels.reshape(top, rows).T
    grid = grid[jax.random.permutation(jax.random.fold_in(own, 1), rows)]
    offset_by = jax.random.randint(jax.random.fold_in(own, 2), (rows, 1), 0, top)
    return jnp.take_along_axis(grid, (jnp.arange(top)[None, :] + offset_by) % top, axis=1)


def portions_of(count, total, limit, skew, full):
    weights = [(1 << 20) // math.isqrt(standing ** skew) + 1 for standing in range(1, count + 1)]
    largest = limit if full else min(limit, max(-(-total // count), total * weights[0] // sum(weights)))
    least = 1 if total - largest >= count - 1 else 0
    holding, spare = [largest] + [least] * (count - 1), total - largest - least * (count - 1)
    while spare > 0:
        movable = [i for i in range(1, count) if holding[i] < largest] or [i for i in range(1, count) if holding[i] < limit]
        whole, budget = sum([weights[i] for i in movable]), spare
        for i in movable:
            extra = min(limit - holding[i], max(1, budget * weights[i] // whole), spare)
            holding[i] = holding[i] + extra
            spare = spare - extra
    return np.array(holding)


def noise(own_key, shape, scale, limit, cuts=(), kind=jnp.bfloat16):
    array = jax.random.normal(own_key, shape, jnp.float32) * scale
    if len(cuts) > 0:
        array = block_scale(own_key, shape, cuts, -0.22, 0.18) * array
    return jnp.clip(array, min=-limit, max=limit).astype(kind)


def setup_inputs(seed: int = 0) -> dict:
    seeds = jax.random.split(jax.random.key(seed), 16)
    block_input = noise(seeds[0], (TOKENS, D), 1.0, 6.0, ((0, 32),))
    cotangent = noise(seeds[1], (TOKENS, D), 1.0, 6.0, ((0, 32),))
    lengths = draw_lengths(jax.random.fold_in(seeds[15], 71), 0)
    routes_keys = jax.random.split(jax.random.fold_in(seeds[3], 1), TOKENS // ROWS)
    routes_turns = jax.random.permutation(jax.random.fold_in(seeds[3], 3), TOKENS // ROWS)
    routes = jax.vmap(lambda own, number: assign_block(jax.random.fold_in(seeds[3], 2), own, number, ROWS, EXPERTS, 2, CAP, 1))(routes_keys, routes_turns).reshape((TOKENS, 2))
    buckets = place_ends(jax.random.randint(seeds[4], (SEQ,), 0, NB), jax.random.fold_in(seeds[4], 1), 0, NB - 1).astype(jnp.int32)
    attn_gain = jnp.clip(1.0 + 0.15 * jax.random.normal(seeds[5], (D,), jnp.float32), 0.25, 1.75).astype(jnp.bfloat16)
    moe_gain = jnp.clip(1.0 + 0.15 * jax.random.normal(seeds[6], (D,), jnp.float32), 0.25, 1.75).astype(jnp.bfloat16)
    query_weight = noise(seeds[7], (D, H * HD), D ** -0.5, 0.21875, ((1, 4),))
    key_weight = noise(seeds[8], (D, H * HD), D ** -0.5, 0.21875, ((1, 4),))
    value_weight = noise(seeds[9], (D, H * HD), D ** -0.5, 0.21875, ((1, 4),))
    output_weight = noise(seeds[10], (H * HD, D), (H * HD // 16) ** -0.5, 0.875, ((0, 4),))
    bias_table = noise(seeds[11], (NB, H), 1.0, 4.0, ((1, 4),))
    router_weight = noise(seeds[12], (D, EXPERTS), D ** -0.5, 0.21875)
    expert_in = noise(seeds[13], (EXPERTS, D, FF), D ** -0.5, 0.21875, ((0, 8), (2, 4)))
    expert_out = noise(seeds[14], (EXPERTS, FF, D), (FF // 4) ** -0.5, 0.21875, ((0, 8), (1, 4)))
    return dict(block_input=block_input, cotangent=cotangent, lengths=lengths, routes=routes, buckets=buckets, attn_gain=attn_gain, moe_gain=moe_gain, query_weight=query_weight, key_weight=key_weight, value_weight=value_weight, output_weight=output_weight, bias_table=bias_table, router_weight=router_weight, expert_in=expert_in, expert_out=expert_out)


EPS = 1e-06
NEG_FILL = -1e+30

@jax.custom_vjp
def low(v):
    return lax.optimization_barrier(v.astype(jnp.bfloat16)).astype(jnp.float32)

@jax.custom_vjp
def low_back(v):
    return v

def low_keep(v):
    return (low(v), None)

def low_pass(kept, grad):
    return (grad,)

def back_keep(v):
    return (v, None)

def back_low(kept, grad):
    return (low(grad),)
low.defvjp(low_keep, low_pass)
low_back.defvjp(back_keep, back_low)

def matmul(left, right):
    return jnp.dot(left, right, precision=lax.Precision.HIGHEST)

def gelu_tanh(values):
    return jax.nn.gelu(values, approximate=True)

def rms_norm(row_values, gain_vec):
    factor = lax.rsqrt(lax.optimization_barrier(jnp.mean(row_values * row_values, axis=-1, keepdims=True)) + EPS)
    return row_values * factor * gain_vec

def attend_one(query_seq, key_seq, value_seq, seq_length, bias_vec):
    positions = jnp.arange(SEQ, dtype=jnp.int32)
    distance = jnp.maximum(positions[:, None] - positions[None, :], 0)
    bias_full = jnp.take(bias_vec.T, distance, axis=1)
    raw_scores = jnp.einsum('qhd,khd->hqk', query_seq, key_seq, precision=lax.Precision.HIGHEST) * HD ** (-0.5) + bias_full
    scores = low_back(raw_scores)
    allowed = (positions[None, :] <= positions[:, None]) & (positions[None, :] < seq_length)
    masked = jnp.where(allowed[None], scores, NEG_FILL)
    log_total = jax.nn.logsumexp(masked, axis=-1, keepdims=True)
    weights = low(jnp.exp(masked - log_total))
    return jnp.einsum('hqk,khd->qhd', weights, value_seq, precision=lax.Precision.HIGHEST)

def expert_one(expert_rows, weight_in, weight_out):
    quarter = FF // N_TENSOR
    copies = low_back(jnp.broadcast_to(expert_rows[None], (N_TENSOR,) + expert_rows.shape))
    part_in = weight_in.reshape(D, N_TENSOR, quarter).transpose(1, 0, 2)
    part_out = weight_out.reshape(N_TENSOR, quarter, D)
    pre_act = low_back(jnp.einsum('qmd,qdf->qmf', copies, part_in, precision=lax.Precision.HIGHEST))
    act_rows = low(gelu_tanh(pre_act))
    part_outs = low(low_back(jnp.einsum('qmf,qfd->qmd', act_rows, part_out, precision=lax.Precision.HIGHEST)))
    return lax.optimization_barrier(jnp.sum(part_outs, axis=0))

def valid_slots(lengths):
    positions = jnp.arange(SEQ, dtype=jnp.int32)
    return (positions[None, :] < lengths[:, None]).reshape(TOKENS)

def forward(block_input, attn_gain, moe_gain, query_weight, key_weight, value_weight, output_weight, bias_table, router_weight, expert_in, expert_out, lengths, routes, buckets):
    valid_mask = valid_slots(lengths)
    hidden_one = low(rms_norm(block_input, attn_gain))
    query_rows = low(low_back(matmul(hidden_one, query_weight)))
    key_rows = low(low_back(matmul(hidden_one, key_weight)))
    value_rows = low(low_back(matmul(hidden_one, value_weight)))
    bias_vec = bias_table[buckets]
    seq_shape = (SEQS, SEQ, H, HD)

    def one_seq(packed):
        return attend_one(packed[0], packed[1], packed[2], packed[3], bias_vec)
    attended = lax.map(jax.checkpoint(one_seq), (query_rows.reshape(seq_shape), key_rows.reshape(seq_shape), value_rows.reshape(seq_shape), lengths))
    head_rows = low(low_back(attended.reshape(TOKENS, H * HD)))
    middle = block_input + low_back(matmul(head_rows, output_weight))
    hidden_two = low(rms_norm(middle, moe_gain))
    logits = matmul(hidden_two, router_weight)
    gate_vals = low(jax.nn.softmax(jnp.take_along_axis(logits, routes, axis=1), axis=-1))
    route_hits = ((routes[:, :, None] == jnp.arange(EXPERTS, dtype=jnp.int32)) & valid_mask[:, None, None]).astype(jnp.int32).reshape(N_DP, ROWS * 2, EXPERTS)
    before = jnp.cumsum(route_hits, axis=1) - route_hits
    slot_index = lax.optimization_barrier(jnp.sum(before * route_hits, axis=2)).reshape(TOKENS, 2)
    group_index = (jnp.arange(TOKENS, dtype=jnp.int32) // ROWS)[:, None]
    slots_all = EXPERTS * N_DP * CAP
    target = jnp.where(valid_mask[:, None], (routes * N_DP + group_index) * CAP + slot_index, slots_all).reshape(TOKENS * 2)
    token_index = jnp.repeat(jnp.arange(TOKENS, dtype=jnp.int32), 2)
    source = jnp.zeros((slots_all,), jnp.int32).at[target].set(token_index, mode='drop')
    filled = jnp.zeros((slots_all,), jnp.float32).at[target].set(1.0, mode='drop')
    dispatched = (hidden_two[source] * filled[:, None]).reshape(EXPERTS, N_DP * CAP, D)

    def one_expert(packed):
        return expert_one(packed[0], packed[1], packed[2])
    expert_outs = lax.map(jax.checkpoint(one_expert), (dispatched, expert_in, expert_out)).reshape(slots_all, D)
    picked = expert_outs[jnp.minimum(target, slots_all - 1)].reshape(TOKENS, 2, D)
    moe_out = low_back(lax.optimization_barrier(jnp.sum(gate_vals[:, :, None] * picked, axis=1)) * valid_mask.astype(jnp.float32)[:, None])
    return middle + moe_out

def reference(block_input, cotangent, lengths, routes, buckets, attn_gain, moe_gain, query_weight, key_weight, value_weight, output_weight, bias_table, router_weight, expert_in, expert_out):

    def run_block(input_f, gain_one, gain_two, query_w, key_w, value_w, output_w, table_w, router_w, in_w, out_w):
        return forward(input_f, gain_one, gain_two, query_w, key_w, value_w, output_w, table_w, router_w, in_w, out_w, lengths, routes, buckets)
    output, pullback = jax.vjp(run_block, block_input.astype(jnp.float32), attn_gain.astype(jnp.float32), moe_gain.astype(jnp.float32), query_weight.astype(jnp.float32), key_weight.astype(jnp.float32), value_weight.astype(jnp.float32), output_weight.astype(jnp.float32), bias_table.astype(jnp.float32), router_weight.astype(jnp.float32), expert_in.astype(jnp.float32), expert_out.astype(jnp.float32))
    grad_out = cotangent.astype(jnp.float32) * valid_slots(lengths).astype(jnp.float32)[:, None]
    input_grad, attn_gain_grad, moe_gain_grad, query_grad, key_grad, value_grad, output_grad, table_grad, router_grad, expert_in_grad, expert_out_grad = pullback(grad_out)
    return (output, input_grad, attn_gain_grad, moe_gain_grad, query_grad, key_grad, value_grad, output_grad, table_grad, router_grad, expert_in_grad, expert_out_grad)
```

```python
import functools

import jax
import jax.numpy as jnp
from jax import lax
from jax.experimental import pallas as pl
from jax.experimental.pallas import tpu as pltpu
from jax.sharding import PartitionSpec as P

EPS = 1e-06
NEG_FILL = -1e30
BF = jnp.bfloat16
F32 = jnp.float32
BLK = 256
HIGHEST = lax.Precision.HIGHEST
GELU_C = 0.7978845608028654
GELU_A = 0.044715


def dot_nt(left, right):
    return lax.dot_general(left, right, (((1,), (1,)), ((), ())), preferred_element_type=F32)


def dot_nn(left, right):
    return lax.dot_general(left, right, (((1,), (0,)), ((), ())), preferred_element_type=F32)


def dot_tn(left, right):
    return lax.dot_general(left, right, (((0,), (0,)), ((), ())), preferred_element_type=F32)


def bias_tiles_kernel(rev_ref, tile_ref, *, heads, blocks):
    for h in range(heads):
        for d in range(blocks):
            first = (blocks - 1 - d) * BLK
            window = jnp.broadcast_to(rev_ref[h : h + 1, first : first + 2 * BLK], (BLK, 2 * BLK))
            turned = pltpu.roll(window, BLK + 1, 1, stride=1, stride_axis=0)
            tile_ref[h, d] = turned[:, :BLK]


def masked_scores(query_blk, key_blk, tile, row_blk, col_blk, length):
    scores = dot_nt(query_blk, key_blk) + tile
    col = lax.broadcasted_iota(jnp.int32, (BLK, BLK), 1)
    allowed = col + col_blk * BLK < length
    if row_blk == col_blk:
        allowed = allowed & (col <= lax.broadcasted_iota(jnp.int32, (BLK, BLK), 0))
    return jnp.where(allowed, scores, NEG_FILL)


def attn_fwd_kernel(
    info_ref, q_ref, k_ref, v_ref, tile_ref, wo_ref, heads_ref, lse_ref, keep_ref, send_ref, *,
    heads, blocks, head_dim,
):
    length = info_ref[0]
    core = info_ref[1]
    scale = head_dim ** (-0.5)
    lane = lax.broadcasted_iota(jnp.int32, (BLK, 128), 1)
    for i in range(blocks):
        rows = slice(i * BLK, (i + 1) * BLK)
        stats = jnp.zeros((BLK, 128), F32)
        for h in range(heads):
            lanes = slice(h * head_dim, (h + 1) * head_dim)
            query_blk = q_ref[rows, lanes] * jnp.asarray(scale, BF)
            parts = []
            for j in range(i + 1):
                parts.append(
                    masked_scores(
                        query_blk,
                        k_ref[j * BLK : (j + 1) * BLK, lanes],
                        tile_ref[h, i - j],
                        i,
                        j,
                        length,
                    )
                )
            top = functools.reduce(jnp.maximum, parts)
            peak = jnp.max(top, axis=1, keepdims=True)
            total = None
            mixed = None
            for j in range(i + 1):
                grown = jnp.exp(parts[j] - peak)
                total = grown if total is None else total + grown
                term = dot_nn(grown.astype(BF), v_ref[j * BLK : (j + 1) * BLK, lanes])
                mixed = term if mixed is None else mixed + term
            sums = jnp.sum(total, axis=1, keepdims=True)
            heads_ref[rows, lanes] = (mixed / sums).astype(BF)
            stats = jnp.where(lane == h, peak + jnp.log(sums), stats)
        lse_ref[rows, :] = stats
        part = dot_nn(heads_ref[rows, :], wo_ref[...]).astype(BF)
        half_rows = slice((i // 2) * BLK, (i // 2 + 1) * BLK)

        @pl.when(core == i % 2)
        def _():
            keep_ref[half_rows, :] = part

        @pl.when(core != i % 2)
        def _():
            send_ref[half_rows, :] = part


def attn_bwd_kernel(
    info_ref, q_ref, k_ref, v_ref, heads_ref, dh_ref, lse_ref, tile_ref,
    dq_ref, dk_ref, dv_ref, dist_ref, acc_ref, dk_acc, dv_acc, *,
    heads, blocks, head_dim,
):
    length = info_ref[0]
    scale = head_dim ** (-0.5)
    ri = lax.broadcasted_iota(jnp.int32, (BLK, BLK), 0)
    ci = lax.broadcasted_iota(jnp.int32, (BLK, BLK), 1)
    flip = (ri + ci == BLK - 1).astype(F32).astype(BF)
    for h in range(heads):
        lanes = slice(h * head_dim, (h + 1) * head_dim)
        for i in range(blocks):
            rows = slice(i * BLK, (i + 1) * BLK)
            query_blk = q_ref[rows, lanes] * jnp.asarray(scale, BF)
            grad_blk = dh_ref[rows, lanes]
            delta = jnp.sum(
                heads_ref[rows, lanes].astype(F32) * grad_blk.astype(F32), axis=1, keepdims=True
            )
            log_total = lse_ref[rows, h : h + 1]
            dq = None
            for j in range(i + 1):
                cols = slice(j * BLK, (j + 1) * BLK)
                key_blk = k_ref[cols, lanes]
                scores = masked_scores(query_blk, key_blk, tile_ref[h, i - j], i, j, length)
                weights = jnp.exp(scores - log_total)
                weight_grad = dot_nt(grad_blk, v_ref[cols, lanes])
                score_grad = weights * (weight_grad - delta)
                score_b = score_grad.astype(BF)
                term = dot_nn(score_b, key_blk)
                dq = term if dq is None else dq + term
                dk_term = dot_tn(score_b, query_blk)
                dv_term = dot_tn(weights.astype(BF), grad_blk)
                if i == j:
                    dk_acc[cols, :] = dk_term
                    dv_acc[cols, :] = dv_term
                else:
                    dk_acc[cols, :] += dk_term
                    dv_acc[cols, :] += dv_term
                if j == 0:
                    acc_ref[i - j] = score_grad
                else:
                    acc_ref[i - j] += score_grad
            dq_ref[rows, lanes] = (dq * scale).astype(BF)
        dk_ref[:, lanes] = dk_acc[...].astype(BF)
        dv_ref[:, lanes] = dv_acc[...].astype(BF)
        for d in range(blocks):
            tile = acc_ref[d]
            high = tile.astype(BF)
            low = (tile - high.astype(F32)).astype(BF)
            turned = dot_nn(flip, high) + dot_nn(flip, low)
            wide = jnp.concatenate([turned, jnp.zeros((BLK, BLK), F32)], axis=1)
            skewed = pltpu.roll(wide, 0, 1, stride=1, stride_axis=0)
            dist_ref[h, d : d + 1, :] = jnp.sum(skewed, axis=0, keepdims=True)


def expert_core_kernel(
    info_ref, h0, hx, hc, hxc, g0, gx, gc, gxc, gate_ref, in_ref, out_ref,
    own_ref, oth_ref, rows_ref, grads_ref, gact_ref, dpre_ref, dgate_ref, *,
    groups, cap, per_half,
):
    step = pl.program_id(0)
    rel = step // per_half
    num = step % per_half
    xh = info_ref[1]
    half = h0.shape[-1]
    near = pl.multiple_of(xh * half, 128)
    far = pl.multiple_of((1 - xh) * half, 128)

    def gather(a_h, b_h, a_g, b_g):
        for g in range(groups):
            span = slice(g * cap, (g + 1) * cap)
            rows_ref[0, span, pl.ds(near, half)] = a_h[g, num]
            rows_ref[0, span, pl.ds(far, half)] = b_h[g, num]
            grads_ref[0, span, pl.ds(near, half)] = a_g[g, num]
            grads_ref[0, span, pl.ds(far, half)] = b_g[g, num]

    @pl.when(rel == 0)
    def _():
        gather(h0, hx, g0, gx)

    @pl.when(rel != 0)
    def _():
        gather(hc, hxc, gc, gxc)

    rows_n = groups * cap
    width = in_ref.shape[-1]
    gate = jnp.broadcast_to(gate_ref[0], (128, rows_n)).T
    gate = jnp.concatenate([gate] * (width // 128), axis=1)
    pre = dot_nn(rows_ref[0], in_ref[0])
    back = dot_nt(grads_ref[0], out_ref[0])
    tanh = jnp.tanh(GELU_C * (pre + GELU_A * pre * pre * pre))
    act = (0.5 * pre * (1.0 + tanh)).astype(BF)
    slope = 0.5 * (1.0 + tanh) + 0.5 * pre * (1.0 - tanh * tanh) * (
        GELU_C * (1.0 + 3.0 * GELU_A * pre * pre)
    )
    act_f = act.astype(F32)
    gact_ref[0] = (act_f * gate).astype(BF)
    dpre = (back * slope * gate).astype(BF)
    dpre_ref[0] = dpre
    ones = jnp.ones((8, width), BF)
    dgate_ref[0] = dot_nt(ones, (act_f * back).astype(BF))
    drows = dot_nt(dpre, in_ref[0]).astype(BF)

    @pl.when(rel == 0)
    def _():
        for g in range(groups):
            own_ref[g, 0] = drows[g * cap : (g + 1) * cap]

    @pl.when(rel != 0)
    def _():
        for g in range(groups):
            oth_ref[g, 0] = drows[g * cap : (g + 1) * cap]


def expert_tail_kernel(
    info_ref, rows_ref, grads_ref, gact_ref, dpre_ref, out_ref, *rest, groups, cap, per_half
):
    own_ref, oth_ref, in_grad_ref, out_grad_ref = rest[-4:]
    rel = pl.program_id(0) // per_half
    outs = dot_nn(gact_ref[0], out_ref[0]).astype(BF)

    @pl.when(rel == 0)
    def _():
        for g in range(groups):
            own_ref[g, 0] = outs[g * cap : (g + 1) * cap]

    @pl.when(rel != 0)
    def _():
        for g in range(groups):
            oth_ref[g, 0] = outs[g * cap : (g + 1) * cap]

    in_grad_ref[0] = dot_tn(rows_ref[0], dpre_ref[0])
    out_grad_ref[0] = dot_tn(gact_ref[0], grads_ref[0])


def expert_maps(chunk, per_half, half_experts):
    def local(s, info):
        return half_experts * (info[0] ^ (s // per_half)) + chunk * per_half + s % per_half

    weight = pl.BlockSpec((1, None, None), lambda s, info: (local(s, info), 0, 0))
    return local, weight


def expert_core(info, hid, cot, gate, expert_in, expert_out, chunk, per_half, half_experts):
    groups, _, cap, half = hid[0].shape
    _, width_in, width = expert_in.shape
    rows_n = groups * cap
    count = 2 * per_half
    local, _ = expert_maps(chunk, per_half, half_experts)
    whole = pl.BlockSpec((groups, per_half, cap, half), lambda s, info: (0, 0, 0, 0))
    row_spec = pl.BlockSpec((1, rows_n, width_in), lambda s, info: (s, 0, 0))
    in_spec = pl.BlockSpec((1, width_in, width), lambda s, info: (local(s, info), 0, 0))
    out_spec = pl.BlockSpec((1, width, width_in), lambda s, info: (local(s, info), 0, 0))
    own = pl.BlockSpec(
        (groups, 1, cap, width_in), lambda s, info: (0, jnp.minimum(s, per_half - 1), 0, 0)
    )
    oth = pl.BlockSpec(
        (groups, 1, cap, width_in), lambda s, info: (0, jnp.maximum(s - per_half, 0), 0, 0)
    )
    return pl.pallas_call(
        functools.partial(expert_core_kernel, groups=groups, cap=cap, per_half=per_half),
        out_shape=(
            jax.ShapeDtypeStruct((groups, per_half, cap, width_in), BF),
            jax.ShapeDtypeStruct((groups, per_half, cap, width_in), BF),
            jax.ShapeDtypeStruct((count, rows_n, width_in), BF),
            jax.ShapeDtypeStruct((count, rows_n, width_in), BF),
            jax.ShapeDtypeStruct((count, rows_n, width), BF),
            jax.ShapeDtypeStruct((count, rows_n, width), BF),
            jax.ShapeDtypeStruct((count, 8, rows_n), F32),
        ),
        grid_spec=pltpu.PrefetchScalarGridSpec(
            num_scalar_prefetch=1,
            grid=(count,),
            in_specs=[whole] * 8
            + [
                pl.BlockSpec((1, 1, rows_n), lambda s, info: (s, 0, 0)),
                in_spec,
                out_spec,
            ],
            out_specs=[
                own,
                oth,
                row_spec,
                row_spec,
                pl.BlockSpec((1, rows_n, width), lambda s, info: (s, 0, 0)),
                pl.BlockSpec((1, rows_n, width), lambda s, info: (s, 0, 0)),
                pl.BlockSpec((1, 8, rows_n), lambda s, info: (s, 0, 0)),
            ],
        ),
        compiler_params=pltpu.CompilerParams(vmem_limit_bytes=56 << 20),
        cost_estimate=pl.CostEstimate(
            flops=6 * count * rows_n * width_in * width,
            bytes_accessed=count * (4 * width * width_in + 10 * rows_n * width_in),
            transcendentals=count * rows_n * width,
        ),
        name="expert_core",
    )(info, *hid, *cot, gate, expert_in, expert_out)


def expert_tail(info, saved, expert_out, partial_grads, chunk, per_half, half_experts, groups, cap):
    rows, grads, gact, dpre = saved
    local_experts, width, width_in = expert_out.shape
    count, rows_n, _ = rows.shape
    local, _ = expert_maps(chunk, per_half, half_experts)
    row_spec = pl.BlockSpec((1, rows_n, width_in), lambda s, info: (s, 0, 0))
    hid_spec = pl.BlockSpec((1, rows_n, width), lambda s, info: (s, 0, 0))
    in_spec = pl.BlockSpec((1, width_in, width), lambda s, info: (local(s, info), 0, 0))
    out_spec = pl.BlockSpec((1, width, width_in), lambda s, info: (local(s, info), 0, 0))
    own = pl.BlockSpec(
        (groups, 1, cap, width_in), lambda s, info: (0, jnp.minimum(s, per_half - 1), 0, 0)
    )
    oth = pl.BlockSpec(
        (groups, 1, cap, width_in), lambda s, info: (0, jnp.maximum(s - per_half, 0), 0, 0)
    )
    extra = [] if partial_grads is None else list(partial_grads)
    return pl.pallas_call(
        functools.partial(expert_tail_kernel, groups=groups, cap=cap, per_half=per_half),
        out_shape=(
            jax.ShapeDtypeStruct((groups, per_half, cap, width_in), BF),
            jax.ShapeDtypeStruct((groups, per_half, cap, width_in), BF),
            jax.ShapeDtypeStruct((local_experts, width_in, width), F32),
            jax.ShapeDtypeStruct((local_experts, width, width_in), F32),
        ),
        grid_spec=pltpu.PrefetchScalarGridSpec(
            num_scalar_prefetch=1,
            grid=(count,),
            in_specs=[row_spec, row_spec, hid_spec, hid_spec, out_spec]
            + [pl.BlockSpec(memory_space=pl.ANY)] * len(extra),
            out_specs=[own, oth, in_spec, out_spec],
        ),
        input_output_aliases={6: 2, 7: 3} if extra else {},
        compiler_params=pltpu.CompilerParams(vmem_limit_bytes=56 << 20),
        cost_estimate=pl.CostEstimate(
            flops=6 * count * rows_n * width_in * width,
            bytes_accessed=count * (10 * width * width_in + 10 * rows_n * width_in),
            transcendentals=0,
        ),
        name="expert_tail",
    )(info, rows, grads, gact, dpre, expert_out, *extra)


def expert_dense(hid, cot, gate, expert_in, expert_out, xh, core):
    def rows_of(pieces):
        def wide(near, far):
            return jnp.concatenate(
                [jnp.where(xh == 0, near, far), jnp.where(xh == 0, far, near)], axis=-1
            )

        mine, other = wide(pieces[0], pieces[1]), wide(pieces[2], pieces[3])
        groups, _, places, feats = mine.shape
        return jnp.stack([mine, other]).reshape(2 * groups * places, feats)

    groups, _, places, _ = hid[0].shape
    rows, grads = rows_of(hid), rows_of(cot)
    gate_col = gate.reshape(2 * groups * places, 1)
    w_in, w_out = expert_in[0], expert_out[0]
    pre = dot_nn(rows, w_in)
    back = dot_nt(grads, w_out)
    act, pull = jax.vjp(lambda v: jax.nn.gelu(v, approximate=True), pre)
    act_f = act.astype(BF).astype(F32)
    gact = (act_f * gate_col).astype(BF)
    dpre = pull(back * gate_col)[0].astype(BF)
    dgate = jnp.sum(act_f * back, axis=1).reshape(2, groups * places)
    shape = (2, groups, 1, places, rows.shape[1])
    drows = dot_nt(dpre, w_in).astype(BF).reshape(shape)
    outs = dot_nn(gact, w_out).astype(BF).reshape(shape)
    return drows, outs, dgate, dot_tn(rows, dpre)[None], dot_tn(gact, grads)[None]


def per_device(
    block_input, cotangent, lengths, routes, buckets, attn_gain, moe_gain, query_weight,
    key_weight, value_weight, output_weight, bias_table, router_weight, expert_in, expert_out,
):
    groups = lax.axis_size("dp")
    own_rows, model_dim = block_input.shape
    seq_len = own_rows * lax.axis_size("tensor")
    half = model_dim // 2
    blocks = seq_len // BLK
    local_heads = bias_table.shape[1]
    head_cols = query_weight.shape[1]
    head_dim = head_cols // local_heads
    experts_all = router_weight.shape[1]
    local_experts = expert_in.shape[0]
    capacity = 3 * seq_len // experts_all
    half_experts = max(local_experts // 2, 1)
    places = capacity if local_experts > 1 else capacity // 2
    chunks = 2 if half_experts % 2 == 0 else 1
    per_half = half_experts // chunks
    assert lax.axis_size("tensor") == 4 and lengths.shape[0] == 1 and own_rows == BLK

    t = lax.axis_index("tensor")
    core = t & 1
    xh = t >> 1
    rank = lax.axis_index("dp")
    core_ring = [(i, i ^ 1) for i in range(4)]
    chip_ring = [(i, i ^ 2) for i in range(4)]

    def via_core(value):
        return lax.ppermute(value, "tensor", core_ring)

    def via_chip(value):
        return lax.ppermute(value, "tensor", chip_ring)

    def pick(bit, first, second):
        return jnp.where(bit == 0, first, second)

    def order(bit, mine, other, axis):
        return jnp.concatenate([pick(bit, mine, other), pick(bit, other, mine)], axis=axis)

    def near_half(value):
        return pick(xh, value[..., :half], value[..., half:])

    def far_half(value):
        return pick(xh, value[..., half:], value[..., :half])

    def weave(mine, other):
        cols = mine.shape[1]
        both = order(
            core, mine.reshape(2, 1, BLK, cols), other.reshape(2, 1, BLK, cols), 1
        )
        return both.reshape(seq_len, cols)

    def rows_split(value):
        four = value.reshape(2, 2, BLK, value.shape[1])
        keep = pick(core, four[:, 0], four[:, 1]).reshape(2 * BLK, value.shape[1])
        send = pick(core, four[:, 1], four[:, 0]).reshape(2 * BLK, value.shape[1])
        return keep, send

    def lanes_split(value):
        lead = value.shape[:-1]
        four = value.reshape(lead + (2, 2, BLK))
        keep = pick(core, four[..., 0, :], four[..., 1, :]).reshape(lead + (2 * BLK,))
        send = pick(core, four[..., 1, :], four[..., 0, :]).reshape(lead + (2 * BLK,))
        return keep, send

    from_chip = via_chip(block_input)
    from_core = via_core(block_input)
    cot_far = via_chip(far_half(cotangent))
    length = lengths[0]
    info_attn = jnp.stack([length, core])
    info_exp = jnp.stack([core, xh])

    positions = jnp.arange(seq_len, dtype=jnp.int32)
    valid_row = positions < length
    expert_ids = jnp.arange(experts_all, dtype=jnp.int32)[:, None]
    routes_t = routes.T
    route_hit = (routes_t[0:1] == expert_ids) | (routes_t[1:2] == expert_ids)
    hit = route_hit & valid_row[None]
    earlier = (positions[:, None] < positions[None, :]).astype(BF)
    before = dot_nn(hit.astype(BF), earlier)
    place = jnp.where(hit, before.astype(jnp.int32), -1)
    place_four = place.reshape(groups, local_experts, seq_len)
    if local_experts > 1:
        place_half = pick(core, place_four[:, :half_experts], place_four[:, half_experts:])
        place_base = 0
    else:
        place_half = place_four
        place_base = core * places
    place_ids = place_base + jnp.arange(places, dtype=jnp.int32)[:, None]
    tables = []
    for j in range(chunks):
        part = place_half[:, j * per_half : (j + 1) * per_half]
        table = (part[:, :, None] == place_ids).astype(BF)
        tables.append(table.reshape(groups * per_half * places, seq_len))

    rev_buckets = buckets[::-1]
    table_ids = jnp.arange(bias_table.shape[0], dtype=jnp.int32)
    rev_hot = (rev_buckets[:, None] == table_ids).astype(BF)
    rev_hot = jnp.concatenate([rev_hot, jnp.broadcast_to(rev_hot[-1:], (BLK, rev_hot.shape[1]))])
    bias_rev = lax.dot_general(
        bias_table, rev_hot, (((0,), (1,)), ((), ())), preferred_element_type=F32
    )
    tiles = pl.pallas_call(
        functools.partial(bias_tiles_kernel, heads=local_heads, blocks=blocks),
        out_shape=jax.ShapeDtypeStruct((local_heads, blocks, BLK, BLK), F32),
        name="bias_tiles",
    )(bias_rev)

    cot_quarter = order(xh, near_half(cotangent), cot_far, 0)
    cot_half = weave(cot_quarter, via_core(cot_quarter))

    def exchange(half_rows, j):
        picked = dot_nn(tables[j], half_rows).astype(BF)
        sent = picked.reshape(groups, per_half, places, half)
        arrived = lax.all_to_all(sent, "dp", 0, 0, tiled=True)
        crossed = via_chip(arrived)
        return arrived, crossed, via_core(arrived), via_core(crossed)

    gain_one = attn_gain.astype(F32)

    def norm_rows(rows):
        rows_f = rows.astype(F32)
        factor = lax.rsqrt(jnp.mean(rows_f * rows_f, axis=-1, keepdims=True) + EPS)
        return (rows_f * factor * gain_one).astype(BF)

    in_near = order(core, block_input, from_core, 0)
    hid_near = norm_rows(in_near)
    in_far = order(core, from_chip, via_core(from_chip), 0)
    hid_far = norm_rows(in_far)
    hidden_one = order(xh, hid_near, hid_far, 0)
    input_all = order(xh, in_near, in_far, 0)

    def project(weight):
        return order(xh, dot_nn(hid_near, weight).astype(BF), dot_nn(hid_far, weight).astype(BF), 0)

    query_rows = project(query_weight)
    key_rows = project(key_weight)
    value_rows = project(value_weight)

    smem = pl.BlockSpec(memory_space=pltpu.SMEM)
    vmem = pl.BlockSpec(memory_space=pltpu.VMEM)
    pair_count = local_heads * blocks * (blocks + 1) // 2
    attn_heads, log_totals, part_keep, part_send = pl.pallas_call(
        functools.partial(attn_fwd_kernel, heads=local_heads, blocks=blocks, head_dim=head_dim),
        out_shape=(
            jax.ShapeDtypeStruct((seq_len, head_cols), BF),
            jax.ShapeDtypeStruct((seq_len, 128), F32),
            jax.ShapeDtypeStruct((2 * BLK, model_dim), BF),
            jax.ShapeDtypeStruct((2 * BLK, model_dim), BF),
        ),
        in_specs=[smem] + [vmem] * 5,
        out_specs=[vmem] * 4,
        cost_estimate=pl.CostEstimate(
            flops=4 * pair_count * BLK * BLK * 256,
            bytes_accessed=8 << 20,
            transcendentals=pair_count * BLK * BLK,
        ),
        name="attn_fwd",
    )(info_attn, query_rows, key_rows, value_rows, tiles, output_weight)

    chip_sum = part_keep.astype(F32) + via_core(part_send).astype(F32)
    crossing = via_chip(far_half(chip_sum).astype(BF))
    input_quarter = near_half(order(xh, block_input, from_chip, 0)).astype(F32)
    middle = input_quarter + near_half(chip_sum) + crossing.astype(F32)
    square_part = jnp.sum(middle * middle, axis=1)
    factor_two = lax.rsqrt((square_part + via_chip(square_part)) / model_dim + EPS)[:, None]
    normed_two = middle * factor_two
    gain_two = near_half(moe_gain).astype(F32)
    hid_quarter = (normed_two * gain_two).astype(BF)
    hid_half = weave(hid_quarter, via_core(hid_quarter))

    cot_pieces = [exchange(cot_half, j) for j in range(chunks)]
    hid_pieces = [exchange(hid_half, j) for j in range(chunks)]

    router_half = pick(xh, router_weight[:half], router_weight[half:])
    logit_part = lax.dot_general(
        router_half, hid_quarter, (((0,), (1,)), ((), ())), preferred_element_type=F32
    )
    logits = logit_part + via_chip(logit_part)
    named, _ = lanes_split(route_hit)
    chosen = jnp.where(named, logits, NEG_FILL)
    grown = jnp.where(named, jnp.exp(chosen - jnp.max(chosen, axis=0, keepdims=True)), 0.0)
    gates_f = grown / jnp.sum(grown, axis=0, keepdims=True)
    gates_b = gates_f.astype(BF)
    gates_other = via_core(gates_b)
    gates_all = order(
        core,
        gates_b.reshape(experts_all, 2, 1, BLK),
        gates_other.reshape(experts_all, 2, 1, BLK),
        2,
    ).reshape(groups, local_experts, seq_len)
    if local_experts > 1:
        gates_half = pick(core, gates_all[:, :half_experts], gates_all[:, half_experts:])
    else:
        gates_half = gates_all
    gates_half = gates_half.astype(F32)
    gate_slots = []
    for j in range(chunks):
        table = tables[j].reshape(groups, per_half, places, seq_len).astype(F32)
        gate_slots.append(
            jnp.sum(table * gates_half[:, j * per_half : (j + 1) * per_half, None], axis=3)
        )
    gate_sent = jnp.concatenate(gate_slots, axis=1)
    gate_near = lax.all_to_all(gate_sent, "dp", 0, 0, tiled=True)
    gate_far = via_core(gate_near)

    def gate_rows(j):
        span = slice(j * per_half, (j + 1) * per_half)
        both = jnp.concatenate([gate_near[:, span], gate_far[:, span]], axis=1)
        return both.transpose(1, 0, 2).reshape(2 * per_half, 1, groups * places)

    def combine(own, oth):
        total = own.astype(F32) + via_core(oth).astype(F32)
        crossed = via_chip(far_half(total).astype(BF))
        summed = (near_half(total) + crossed.astype(F32)).astype(BF)
        back = lax.all_to_all(summed, "dp", 0, 0, tiled=True)
        return back.reshape(groups * per_half * places, half)

    row_grads, out_rows, gate_sums = [], [], []
    if local_experts > 1:
        saved = []
        for j in range(chunks):
            own, oth, rows, grads, gact, dpre, dgate = expert_core(
                info_exp, hid_pieces[j], cot_pieces[j], gate_rows(j), expert_in, expert_out,
                j, per_half, half_experts,
            )
            row_grads.append((own, oth))
            gate_sums.append(dgate[:, 0])
            saved.append((rows, grads, gact, dpre))
        weight_grads = None
        for j in range(chunks):
            own, oth, in_grad, out_grad = expert_tail(
                info_exp, saved[j], expert_out, weight_grads, j, per_half, half_experts,
                groups, places,
            )
            out_rows.append((own, oth))
            weight_grads = (in_grad, out_grad)
    else:
        drows, outs, dgate, in_grad, out_grad = expert_dense(
            hid_pieces[0], cot_pieces[0], gate_rows(0), expert_in, expert_out, xh, core
        )
        row_grads.append((drows[0], drows[1]))
        out_rows.append((outs[0], outs[1]))
        gate_sums.append(dgate)
        weight_grads = (in_grad, out_grad)

    def token_sum(returned):
        total = None
        for j in range(chunks):
            term = dot_tn(tables[j], returned[j])
            total = term if total is None else total + term
        keep, send = rows_split(total)
        return keep + via_core(send)

    grad_quarter = token_sum([combine(*pair) for pair in row_grads])

    gate_own = jnp.concatenate([part[:per_half] for part in gate_sums])
    gate_oth = jnp.concatenate([part[per_half:] for part in gate_sums])
    gate_sum = gate_own + via_core(gate_oth)
    gate_sum = gate_sum + via_chip(gate_sum)
    gate_sum = gate_sum.reshape(half_experts, groups, places).transpose(1, 0, 2)
    gate_back = lax.all_to_all(gate_sum, "dp", 0, 0, tiled=True)
    gate_tokens = []
    for j in range(chunks):
        table = tables[j].reshape(groups, per_half, places, seq_len).astype(F32)
        gate_tokens.append(
            jnp.sum(table * gate_back[:, j * per_half : (j + 1) * per_half, :, None], axis=2)
        )
    gate_keep, gate_send = lanes_split(jnp.concatenate(gate_tokens, axis=1))
    gate_other = via_core(gate_send)
    if local_experts > 1:
        gate_grad = order(core, gate_keep, gate_other, 1)
    else:
        gate_grad = gate_keep + gate_other
    gate_grad = gate_grad.reshape(experts_all, 2 * BLK)
    logit_grad = gates_f * (gate_grad - jnp.sum(gates_f * gate_grad, axis=0, keepdims=True))
    router_f = router_half.astype(F32)
    grad_quarter = grad_quarter + lax.dot_general(
        logit_grad, router_f, (((0,), (1,)), ((), ())), precision=HIGHEST
    )
    router_part = lax.dot_general(
        hid_quarter.astype(F32), logit_grad, (((0,), (1,)), ((), ())), precision=HIGHEST
    )
    gain_two_part = jnp.sum(grad_quarter * normed_two, axis=0)

    scaled_two = grad_quarter * gain_two
    mean_part = jnp.sum(scaled_two * normed_two, axis=1)
    mean_two = (mean_part + via_chip(mean_part))[:, None] / model_dim
    valid_keep, _ = lanes_split(valid_row[None])
    grad_out = cot_quarter.astype(F32) * valid_keep.reshape(2 * BLK, 1).astype(F32)
    middle_grad = grad_out + factor_two * (scaled_two - normed_two * mean_two)
    middle_b = middle_grad.astype(BF)
    middle_rows = order(xh, middle_b, via_chip(middle_b), 1)
    attn_back = weave(middle_rows, via_core(middle_rows))

    heads_grad = dot_nt(attn_back, output_weight).astype(BF)
    output_part = dot_tn(attn_heads, attn_back)
    dquery, dkey, dvalue, dist = pl.pallas_call(
        functools.partial(attn_bwd_kernel, heads=local_heads, blocks=blocks, head_dim=head_dim),
        out_shape=(
            jax.ShapeDtypeStruct((seq_len, head_cols), BF),
            jax.ShapeDtypeStruct((seq_len, head_cols), BF),
            jax.ShapeDtypeStruct((seq_len, head_cols), BF),
            jax.ShapeDtypeStruct((local_heads, blocks, 2 * BLK), F32),
        ),
        in_specs=[smem] + [vmem] * 7,
        out_specs=[vmem] * 4,
        scratch_shapes=[
            pltpu.VMEM((blocks, BLK, BLK), F32),
            pltpu.VMEM((seq_len, head_dim), F32),
            pltpu.VMEM((seq_len, head_dim), F32),
        ],
        cost_estimate=pl.CostEstimate(
            flops=10 * pair_count * BLK * BLK * 256,
            bytes_accessed=8 << 20,
            transcendentals=pair_count * BLK * BLK,
        ),
        name="attn_bwd",
    )(info_attn, query_rows, key_rows, value_rows, attn_heads, heads_grad, log_totals, tiles)

    query_part = dot_tn(hidden_one, dquery)
    key_part = dot_tn(hidden_one, dkey)
    value_part = dot_tn(hidden_one, dvalue)
    input_part = (
        dot_nt(dquery, query_weight) + dot_nt(dkey, key_weight) + dot_nt(dvalue, value_weight)
    )
    input_f = input_all.astype(F32)
    factor_all = lax.rsqrt(jnp.mean(input_f * input_f, axis=-1, keepdims=True) + EPS)
    gain_one_part = jnp.sum(input_part * (input_f * factor_all), axis=0)

    rev_index = jnp.concatenate([rev_buckets, jnp.broadcast_to(rev_buckets[-1:], (BLK,))])
    table_part = None
    for d in range(blocks):
        first = (blocks - 1 - d) * BLK
        window = (rev_index[None, first : first + 2 * BLK] == table_ids[:, None]).astype(F32)
        term = lax.dot_general(
            window, dist[:, d], (((1,), (1,)), ((), ())), precision=HIGHEST
        )
        table_part = term if table_part is None else table_part + term

    keep_rows, send_rows = rows_split(input_part)
    chip_rows = keep_rows + via_core(send_rows.astype(BF)).astype(F32)
    own_part = pick(xh, chip_rows[:BLK], chip_rows[BLK:])
    other_part = pick(xh, chip_rows[BLK:], chip_rows[:BLK])
    hidden_one_grad = own_part + via_chip(other_part.astype(BF)).astype(F32)
    own_input = block_input.astype(F32)
    factor_own = lax.rsqrt(jnp.mean(own_input * own_input, axis=-1, keepdims=True) + EPS)
    normed_own = own_input * factor_own
    scaled_one = hidden_one_grad * gain_one
    own_middle = pick(xh, middle_rows[:BLK], middle_rows[BLK:]).astype(F32)
    input_grad = own_middle + factor_own * (
        scaled_one - normed_own * jnp.mean(scaled_one * normed_own, axis=-1, keepdims=True)
    )

    out_quarter = middle + token_sum([combine(*pair) for pair in out_rows])
    out_mine = pick(xh, out_quarter[:BLK], out_quarter[BLK:])
    out_sent = pick(xh, out_quarter[BLK:], out_quarter[:BLK])
    block_output = order(xh, out_mine, via_chip(out_sent), 1)

    bits = [b for b in range(groups.bit_length() - 1)]

    def pair_up(value, bit):
        return lax.ppermute(value, "dp", [(i, i ^ (1 << bit)) for i in range(groups)])

    def small_sum(value):
        for bit in bits:
            value = value + pair_up(value, bit)
        return value

    def large_sum(value, sequence):
        for bit in sequence:
            rows = value.shape[0] // 2
            mine = (rank >> bit) & 1
            keep = pick(mine, value[:rows], value[rows:])
            send = pick(mine, value[rows:], value[:rows])
            value = keep + pair_up(send.astype(BF), bit).astype(F32)
        value = value.astype(BF)
        for bit in reversed(sequence):
            value = order((rank >> bit) & 1, value, pair_up(value, bit), 0)
        return value.astype(F32)

    slice_cols = model_dim // 4

    def tensor_slice(value):
        keep = pick(core, value[:slice_cols], value[slice_cols:])
        send = pick(core, value[slice_cols:], value[:slice_cols])
        return keep + via_core(send)

    router_quarter = small_sum(tensor_slice(router_part))
    gain_two_grad = small_sum(tensor_slice(gain_two_part))
    gain_one_near = gain_one_part + via_core(gain_one_part)
    gain_one_sum = gain_one_near + via_chip(gain_one_near)
    gain_one_grad = small_sum(lax.dynamic_slice_in_dim(gain_one_sum, t * slice_cols, slice_cols))
    table_grad = small_sum(table_part)
    output_grad = large_sum(output_part, bits)
    query_grad = large_sum(query_part, bits)
    key_grad = large_sum(key_part, bits[1:2] + bits[:1] + bits[2:])
    value_grad = large_sum(value_part, bits[1:2] + bits[:1] + bits[2:])
    return (
        block_output,
        input_grad,
        gain_one_grad,
        gain_two_grad,
        query_grad,
        key_grad,
        value_grad,
        output_grad,
        table_grad,
        router_quarter,
        weight_grads[0],
        weight_grads[1],
    )


def solution(mesh):
    placed = (
        P(("dp", "tensor"), None),
        P(("dp", "tensor"), None),
        P("dp"),
        P("dp", None),
        P(),
        P(),
        P(),
        P(None, "tensor"),
        P(None, "tensor"),
        P(None, "tensor"),
        P("tensor", None),
        P(None, "tensor"),
        P(),
        P("dp", None, "tensor"),
        P("dp", "tensor", None),
    )
    return jax.shard_map(
        per_device,
        mesh=mesh,
        in_specs=placed,
        out_specs=(
            P(("dp", "tensor"), None),
            P(("dp", "tensor"), None),
            P("tensor"),
            P("tensor"),
            P(None, "tensor"),
            P(None, "tensor"),
            P(None, "tensor"),
            P("tensor", None),
            P(None, "tensor"),
            P("tensor", None),
            P("dp", None, "tensor"),
            P("dp", "tensor", None),
        ),
        check_vma=False,
    )
```
